512 devices in a mesh: rows: 16 (over z), tm: 32 (over x, y, core).
Axes of the slice: x: 4, y: 4, z: 16, core: 2. Of those that a mesh axis runs over, the one named last changes fastest.
Arguments:
- jacobian: bfloat16 [64, 6144, 512], P('tm', 'rows'), may hold values from -3 to 3
- rhs: bfloat16 [64, 6144], P('tm', 'rows'), may hold values from -6 to 6
- forget: float32 [64], P('tm'), may hold values from 0.99 to 1
- restart: int32 [64], P('tm'), may hold values 0 or 1
Outputs:
- factor: float32 [64, 512, 512], P('tm', 'rows')
- state: float32 [64, 512], P('tm', 'rows')
The draws below stay inside these ranges and needn't reach their ends.
All inputs are finite; a program needn't handle non-finite values. No bound on the sum of `restart` on one device may be relied on, other than what follows from the above.
Results may differ from the reference program's by a relative error of at most 0.0003.
Values sent between devices are 32-bit elements; how exact they have to be, the bound alone decides.
No kernel may reach another device: no remote copies, remote signals or barrier semaphores. Data moves between devices by JAX's collectives and lax.ppermute only.
A program may use at most 128 MiB of HBM per device.

```python
import math
import jax
import jax.numpy as jnp
from jax import lax

W = 512
SEGS = 64
ROWS = 6144


def mixing_matrix(key, lowest):
    scale_key, jitter_key = jax.random.split(jax.random.fold_in(key, 11))
    column_scales = jnp.exp(jax.random.uniform(scale_key, (W,), jnp.float32, math.log(lowest), 0.0))
    jitter = jnp.clip(jax.random.normal(jitter_key, (W, W), jnp.float32), -4.0, 4.0) * (0.25 / math.sqrt(W))
    return column_scales[:, None] * (jnp.eye(W, dtype=jnp.float32) + jitter)


def draw_jacobian(key, part):
    lowest = 0.15
    mixing = mixing_matrix(key, lowest)
    segment_keys = jax.random.split(jax.random.fold_in(key, 7), SEGS)

    def one_segment(segment_key):
        latent_key = jax.random.fold_in(segment_key, 0)
        latent = jnp.clip(jax.random.normal(latent_key, (ROWS, W), jnp.float32), -5.0, 5.0)
        mixed = jnp.dot(latent, mixing, precision=lax.Precision.HIGHEST)
        return mixed * jnp.float32(1.0 / math.sqrt(ROWS))
    return lax.map(one_segment, segment_keys).astype(jnp.bfloat16)


def plant(entries, rng, smallest, largest):
    longest = entries.shape.index(max(entries.shape))
    spots = []
    for shift in (0, 1):
        where = [jax.random.randint(jax.random.fold_in(rng, axis), (), 0, length) for axis, length in enumerate(entries.shape)]
        where[longest] = (where[longest] + shift) % entries.shape[longest]
        spots.append(tuple(where))
    return entries.at[spots[0]].set(smallest).at[spots[1]].set(largest)


def level_of(rng, extent, pieces, low, largest):
    def one(dim, shards_of):
        draws = jax.random.uniform(jax.random.fold_in(jax.random.fold_in(rng, 6), dim), (shards_of,), jnp.float32, low / len(pieces), largest / len(pieces))
        return jnp.repeat(jnp.exp(draws), extent[dim] // shards_of).reshape((-1,) + (1,) * (len(extent) - dim - 1))

    loudness = one(*pieces[0])
    for cut in pieces[1:]:
        loudness = loudness * one(*cut)
    return loudness


def gaussian(rng, extent, width, most, shards=(), kind=jnp.bfloat16):
    drawn = width * jax.random.normal(rng, extent, jnp.float32)
    if shards:
        drawn = drawn * level_of(rng, extent, shards, -0.22, 0.18)
    return jnp.clip(drawn, -most, most).astype(kind)


def setup_inputs(seed: int = 0) -> dict:
    streams_of = jax.random.split(jax.random.key(seed), 5)
    return {
        "jacobian": draw_jacobian(jax.random.fold_in(streams_of[4], 71), 0),
        "rhs": gaussian(streams_of[1], (SEGS, ROWS), 1.0, 6.0, ((0, 32), (1, 16))),
        "forget": jnp.clip(jnp.exp(math.log(1.0) - 0.0100503262 * jax.random.uniform(streams_of[2], (SEGS,), jnp.float32) ** level_of(streams_of[2], (SEGS,), ((0, 32),), -0.2, 0.2)), 0.99, 1.0),
        "restart": plant((jax.random.randint(streams_of[3], (SEGS,), 0, 16) < 1).astype(jnp.int32), jax.random.fold_in(streams_of[3], 1), 0, 1),
    }


def segment_terms(pair):
    block, values = pair
    information = jnp.dot(block.T.astype(jnp.float32), block.astype(jnp.float32), preferred_element_type=jnp.float32)
    gradient = jnp.dot(values.astype(jnp.float32), block.astype(jnp.float32), preferred_element_type=jnp.float32)
    return (information, gradient)

def solve_one(pair):
    matrix, vector = pair
    lower_factor = jnp.linalg.cholesky(matrix)
    middle = jax.scipy.linalg.solve_triangular(lower_factor, vector, lower=True)
    result = jax.scipy.linalg.solve_triangular(lower_factor, middle, lower=True, trans=1)
    return (lower_factor.T, result)

def reference(jacobian, rhs, forget, restart):
    decays = forget * (1.0 - 0.2 * restart.astype(jnp.float32))
    information, gradient = lax.map(segment_terms, (jacobian, rhs))

    def advance(carry, inputs):
        matrix, vector = carry
        decay_now, info_now, grad_now = inputs
        matrix = decay_now * matrix + info_now
        vector = decay_now * vector + grad_now
        return ((matrix, vector), (matrix, vector))
    start = (jnp.zeros((W, W), jnp.float32), jnp.zeros((W,), jnp.float32))
    unused, posts = lax.scan(advance, start, (decays, information, gradient))
    factor, state = lax.map(solve_one, posts)
    return (factor, state)
```

```python
import jax
import jax.numpy as jnp
from jax import lax
from jax.experimental import pallas as pl
from jax.experimental.pallas import tpu as pltpu
from jax.sharding import PartitionSpec as P

f32 = jnp.float32
B = 128
HIGH = lax.Precision.HIGHEST
VM = pl.BlockSpec(memory_space=pltpu.VMEM)
SM = pl.BlockSpec(memory_space=pltpu.SMEM)
PARAMS = pltpu.CompilerParams(vmem_limit_bytes=48 << 20)


def block_list(nb):
    return [(b, c) for b in range(nb) for c in range(b, nb)]


def tile_array(*lead):
    return jax.ShapeDtypeStruct(tuple(lead) + (8, B), f32)


def pack_kernel(z_ref, jac_ref, rhs_ref, own, up, down, up2, down2, parts):
    z = z_ref[0]
    segs, rows, width = jac_ref.shape
    nb = width // B
    blocks = block_list(nb)
    last = segs * len(blocks)
    for p in range(4):
        for a in range(4):
            parts[p, a, last] = jnp.zeros((8, B), f32)
    grads = []
    for s in range(segs):
        jac = jac_ref[s]
        for b in range(nb):
            info = lax.dot_general(
                jac[:, b * B:(b + 1) * B], jac[:, b * B:],
                (((0,), (0,)), ((), ())), preferred_element_type=f32)
            for c in range(b, nb):
                tile = s * len(blocks) + blocks.index((b, c))
                piece = info[:, (c - b) * B:(c - b + 1) * B].reshape(4, 4, 8, B)
                for q in range(4):
                    p = lax.rem(q + 16 - z, 4)
                    for a in range(4):
                        parts[p, a, tile] = piece[a, q]
        grads.append(jnp.dot(rhs_ref[...], jac, preferred_element_type=f32)[s:s + 1])
    p = lax.rem(16 - z, 4)
    for s in range(segs):
        for b in range(nb):
            parts[p, 0, last, pl.ds(s * nb + b, 1), :] = grads[s][:, b * B:(b + 1) * B]
    own[...] = parts[0]
    up[...] = parts[1]
    up2[...] = parts[2, 0:2]
    down2[...] = parts[2, 2:4]
    down[...] = parts[3]


def first_sum_kernel(z_ref, own, up, down, up2, down2, mine, plus, minus, far, total):
    h = lax.div(z_ref[0], 4)
    near = own[...] + up[...] + down[...]
    total[0:2] = near[0:2] + up2[...]
    total[2:4] = near[2:4] + down2[...]
    mine[...] = total[h]
    plus[...] = total[lax.rem(h + 1, 4)]
    minus[...] = total[lax.rem(h + 3, 4)]
    far[...] = total[lax.rem(h + 2, 4)]


def second_sum_kernel(decay_ref, mine, plus, minus, far, out, flat):
    total = (mine[...] + plus[...]) + (minus[...] + far[...])
    half = (total.shape[0] - 1) // 2
    for s in range(2):
        flat[s, 0:8 * half] = total[s * half:(s + 1) * half].reshape(8 * half, B)
        flat[s, 8 * half:8 * half + 4] = total[2 * half, 4 * s:4 * s + 4]
        flat[s, 8 * half + 4:] = jnp.zeros((flat.shape[1] - 8 * half - 4, B), f32)
    for t in range(out.shape[0]):
        for s in range(2):
            out[t, 3 * s:3 * s + 3] = flat[s, 3 * t:3 * t + 3]
            out[t, 6 + s:7 + s] = jnp.full((1, B), decay_ref[s], f32)


def scan_kernel(chunks, out):
    now = jnp.zeros((3, B), f32)
    for t in range(chunks.shape[0]):
        for s in range(2):
            now = chunks[t, 6 + s:7 + s] * now + chunks[t, 3 * s:3 * s + 3]
            out[t, 3 * s:3 * s + 3] = now
        out[t, 6:8] = jnp.zeros((2, B), f32)


def unpack_kernel(chunks, out, flat):
    half = (out.shape[0] - 1) // 2
    for t in range(chunks.shape[0]):
        for s in range(2):
            flat[s, 3 * t:3 * t + 3] = chunks[t, 3 * s:3 * s + 3]
    for s in range(2):
        out[s * half:(s + 1) * half] = flat[s, 0:8 * half].reshape(half, 8, B)
        out[2 * half, 4 * s:4 * s + 4] = flat[s, 8 * half:8 * half + 4]


def stack_kernel(mine, below, above, far, full, low, high):
    full[0] = below[...]
    full[1] = mine[...]
    full[2] = above[...]
    full[3] = far[...]
    low[0] = below[...]
    low[1] = mine[...]
    high[0] = mine[...]
    high[1] = above[...]


def spread(row):
    return jnp.broadcast_to(row, (8, B))


def invert_factor(rows, lane, sub):
    groups = len(rows)
    for j in range(groups):
        o = 8 * j
        top = rows[j]
        cols = [jnp.broadcast_to(top[:, o + m:o + m + 1], (8, B)) for m in range(8)]
        inside = (lane >= o) & (lane < o + 8)
        d = []
        for m in range(8):
            unit = jnp.where(lane == o + m, 1.0, 0.0)
            d.append(jnp.where(inside, unit, spread(top[m:m + 1])))
        low = {}
        rs = []
        u = []
        for k in range(8):
            r = lax.rsqrt(spread(cols[k][k:k + 1]))
            rs.append(r)
            col = cols[k] * r
            u.append(d[k] * r)
            for m in range(k + 1, 8):
                low[m, k] = spread(col[m:m + 1])
                cols[m] = cols[m] - col * low[m, k]
                d[m] = d[m] - low[m, k] * u[k]
        w = [None] * 8
        for m in range(7, -1, -1):
            acc = u[m]
            for k in range(m + 1, 8):
                acc = acc - low[k, m] * w[k]
            w[m] = acc * rs[m]
        for i in range(j + 1, groups):
            old = rows[i]
            new = jnp.where(inside, 0.0, old)
            for m in range(8):
                new = new - jnp.broadcast_to(old[:, o + m:o + m + 1], (8, B)) * w[m]
            rows[i] = new
        merged = u[0]
        for m in range(1, 8):
            merged = jnp.where(sub == m, u[m], merged)
        rows[j] = merged
    return rows


def solve_kernel(z_ref, own, up, down, up2, down2, factor, state, mat, upper, inv, vec, sol):
    z = z_ref[0]
    segs, width = mat.shape[0], mat.shape[1]
    nb = width // B
    blocks = block_list(nb)
    nblk = len(blocks)
    lane = lax.broadcasted_iota(jnp.int32, (8, B), 1)
    sub = lax.broadcasted_iota(jnp.int32, (8, B), 0)
    row_i = lax.broadcasted_iota(jnp.int32, (B, B), 0)
    col_i = lax.broadcasted_iota(jnp.int32, (B, B), 1)
    row_w = lax.broadcasted_iota(jnp.int32, (B, width), 0)
    col_w = lax.broadcasted_iota(jnp.int32, (B, width), 1)
    mat[...] = jnp.zeros(mat.shape, f32)
    vec[...] = jnp.zeros(vec.shape, f32)
    sol[...] = jnp.zeros(sol.shape, f32)

    def place(piece, source, shift):
        g = lax.rem(z + (source + shift + 32), 16)
        for s in range(segs):
            for i, (b, c) in enumerate(blocks):
                at = pl.multiple_of(b * B + g * 8, 8)
                mat[s, pl.ds(at, 8), c * B:(c + 1) * B] = piece[s * nblk + i]

        @pl.when(g == 0)
        def _():
            for s in range(segs):
                for b in range(nb):
                    vec[s, 0:1, b * B:(b + 1) * B] = piece[segs * nblk, s * nb + b:s * nb + b + 1]

    shifts = (-4, 0, 4, 8)
    for ref, source in ((own, 0), (up, -1), (down, 1)):
        for i in range(4):
            place(ref.at[i], source, shifts[i])
    for i in range(2):
        place(up2.at[i], -2, (-4, 0)[i])
        place(down2.at[i], 2, (0, 4)[i])

    def step(b, carry):
        at = pl.multiple_of(b * B, B)
        groups = B // 8
        found = []
        for s in range(segs):
            diag = mat[s, pl.ds(at, B), pl.ds(at, B)]
            found.append([diag[8 * i:8 * i + 8] for i in range(groups)])
        for s in range(segs):
            rows = invert_factor(found[s], lane, sub)
            full = jnp.concatenate(rows, axis=0)
            inv[s, b] = jnp.where(col_i <= row_i, full, 0.0)
        for s in range(segs):
            left = inv[s, b]
            panel = jnp.dot(left, mat[s, pl.ds(at, B), :], precision=HIGH, preferred_element_type=f32)
            panel = jnp.where(col_w >= row_w + at, panel, 0.0)
            upper[s, pl.ds(at, B), :] = panel
            y = lax.dot_general(vec[s, :, pl.ds(at, B)], left, (((1,), (1,)), ((), ())),
                                precision=HIGH, preferred_element_type=f32)
            sol[s, :, pl.ds(at, B)] = y
            vec[s] = vec[s] - jnp.dot(y, panel, precision=HIGH, preferred_element_type=f32)
            mat[s] = mat[s] - lax.dot_general(panel, panel, (((0,), (0,)), ((), ())),
                                              precision=HIGH, preferred_element_type=f32)
        return carry

    lax.fori_loop(0, nb, step, 0)

    vec[...] = jnp.zeros(vec.shape, f32)
    for b in range(nb - 1, -1, -1):
        for s in range(segs):
            y = sol[s, :, b * B:(b + 1) * B]
            if b < nb - 1:
                y = y - lax.dot_general(
                    vec[s, :, (b + 1) * B:], upper[s, b * B:(b + 1) * B, (b + 1) * B:],
                    (((1,), (1,)), ((), ())), precision=HIGH, preferred_element_type=f32)
            vec[s, :, b * B:(b + 1) * B] = jnp.dot(y, inv[s, b], precision=HIGH, preferred_element_type=f32)
    share = factor.shape[1]
    start = pl.multiple_of(z * share, share)
    for s in range(segs):
        factor[s] = upper[s, pl.ds(start, share), :]
        state[s:s + 1, :] = vec[s, 0:1, :]


def shifted(value, by):
    count = lax.axis_size("rows")
    return lax.ppermute(value, "rows", [(i, (i + by) % count) for i in range(count)])


def on_device(jacobian, rhs, forget, restart):
    segs, rows, width = jacobian.shape
    nb = width // B
    tiles = segs * len(block_list(nb)) + 1
    tms = lax.axis_size("tm")
    z = lax.axis_index("rows")
    z_now = z.astype(jnp.int32).reshape(1)
    share = width // lax.axis_size("rows")
    decays = forget * (1.0 - 0.2 * restart.astype(f32))

    four, two, one = tile_array(4, tiles), tile_array(2, tiles), tile_array(tiles)
    own, up, down, up2, down2 = pl.pallas_call(
        pack_kernel, out_shape=[four, four, four, two, two],
        in_specs=[SM, VM, VM], out_specs=[VM] * 5,
        scratch_shapes=[pltpu.VMEM((4, 4, tiles, 8, B), f32)],
        compiler_params=PARAMS, name="pack")(z_now, jacobian, rhs)
    up, down, up2, down2 = shifted(up, 1), shifted(down, -1), shifted(up2, 2), shifted(down2, -2)
    mine, plus, minus, far = pl.pallas_call(
        first_sum_kernel, out_shape=[one] * 4,
        in_specs=[SM] + [VM] * 5, out_specs=[VM] * 4,
        scratch_shapes=[pltpu.VMEM((4, tiles, 8, B), f32)],
        compiler_params=PARAMS, name="first_sum")(z_now, own, up, down, up2, down2)
    plus, minus, far = shifted(plus, 4), shifted(minus, -4), shifted(far, 8)
    chunks = pl.pallas_call(
        second_sum_kernel, out_shape=tile_array(tms),
        in_specs=[SM] + [VM] * 4, out_specs=VM,
        scratch_shapes=[pltpu.VMEM((2, 3 * tms, B), f32)],
        compiler_params=PARAMS, name="second_sum")(decays, mine, plus, minus, far)
    chunks = lax.all_to_all(chunks, "tm", 0, 0)
    chunks = pl.pallas_call(
        scan_kernel, out_shape=tile_array(tms), in_specs=[VM], out_specs=VM,
        compiler_params=PARAMS, name="scan")(chunks)
    chunks = lax.all_to_all(chunks, "tm", 0, 0)
    mine = pl.pallas_call(
        unpack_kernel, out_shape=one, in_specs=[VM], out_specs=VM,
        scratch_shapes=[pltpu.VMEM((2, 3 * tms, B), f32)],
        compiler_params=PARAMS, name="unpack")(chunks)
    below, above, far = shifted(mine, 4), shifted(mine, -4), shifted(mine, 8)
    own, low, high = pl.pallas_call(
        stack_kernel, out_shape=[four, two, two], in_specs=[VM] * 4, out_specs=[VM] * 3,
        compiler_params=PARAMS, name="stack")(mine, below, above, far)
    up, down, up2, down2 = shifted(own, 1), shifted(own, -1), shifted(low, 2), shifted(high, -2)
    factor, state = pl.pallas_call(
        solve_kernel,
        out_shape=[jax.ShapeDtypeStruct((segs, share, width), f32), jax.ShapeDtypeStruct((segs, width), f32)],
        in_specs=[SM] + [VM] * 5, out_specs=[VM] * 2,
        scratch_shapes=[
            pltpu.VMEM((segs, width, width), f32), pltpu.VMEM((segs, width, width), f32),
            pltpu.VMEM((segs, nb, B, B), f32), pltpu.VMEM((segs, 8, width), f32),
            pltpu.VMEM((segs, 8, width), f32)],
        compiler_params=PARAMS, name="solve")(z_now, own, up, down, up2, down2)
    return (factor, lax.dynamic_slice_in_dim(state, z * share, share, 1))


def solution(mesh):
    in_specs = (P("tm", "rows", None), P("tm", "rows"), P("tm"), P("tm"))
    out_specs = (P("tm", "rows", None), P("tm", "rows"))
    return jax.shard_map(
        on_device, mesh=mesh, in_specs=in_specs, out_specs=out_specs, check_vma=False
    )
```

```python
import jax
import jax.numpy as jnp
from jax import lax
from jax.experimental import pallas as pl
from jax.experimental.pallas import tpu as pltpu
from jax.sharding import Mesh, PartitionSpec as P

f32 = jnp.float32
B = 128
ROWS = ("pair", "side")
HIGH = lax.Precision.HIGHEST
VM = pl.BlockSpec(memory_space=pltpu.VMEM)
SM = pl.BlockSpec(memory_space=pltpu.SMEM)
PARAMS = pltpu.CompilerParams(vmem_limit_bytes=48 << 20)


def block_list(nb):
    return [(b, c) for b in range(nb) for c in range(b, nb)]


def tile_array(*lead):
    return jax.ShapeDtypeStruct(tuple(lead) + (8, B), f32)


def pack_kernel(z_ref, jac_ref, rhs_ref, own, up, down, up2, down2, parts):
    z = z_ref[0]
    segs, rows, width = jac_ref.shape
    nb = width // B
    blocks = block_list(nb)
    last = segs * len(blocks)
    for p in range(4):
        for a in range(4):
            parts[p, a, last] = jnp.zeros((8, B), f32)
    grads = []
    for s in range(segs):
        jac = jac_ref[s]
        for b in range(nb):
            info = lax.dot_general(
                jac[:, b * B:(b + 1) * B], jac[:, b * B:],
                (((0,), (0,)), ((), ())), preferred_element_type=f32)
            for c in range(b, nb):
                tile = s * len(blocks) + blocks.index((b, c))
                piece = info[:, (c - b) * B:(c - b + 1) * B].reshape(4, 4, 8, B)
                for q in range(4):
                    p = lax.rem(q + 16 - z, 4)
                    for a in range(4):
                        parts[p, a, tile] = piece[a, q]
        grads.append(jnp.dot(rhs_ref[...], jac, preferred_element_type=f32)[s:s + 1])
    p = lax.rem(16 - z, 4)
    for s in range(segs):
        for b in range(nb):
            parts[p, 0, last, pl.ds(s * nb + b, 1), :] = grads[s][:, b * B:(b + 1) * B]
    own[...] = parts[0]
    up[...] = parts[1]
    up2[...] = parts[2, 0:2]
    down2[...] = parts[2, 2:4]
    down[...] = parts[3]


def first_sum_kernel(z_ref, own, up, down, up2, down2, mine, plus, minus, far, total):
    h = lax.div(z_ref[0], 4)
    near = own[...] + up[...] + down[...]
    total[0:2] = near[0:2] + up2[...]
    total[2:4] = near[2:4] + down2[...]
    mine[...] = total[h]
    plus[...] = total[lax.rem(h + 1, 4)]
    minus[...] = total[lax.rem(h + 3, 4)]
    far[...] = total[lax.rem(h + 2, 4)]


def second_sum_kernel(decay_ref, mine, plus, minus, far, out, flat):
    total = (mine[...] + plus[...]) + (minus[...] + far[...])
    half = (total.shape[0] - 1) // 2
    for s in range(2):
        flat[s, 0:8 * half] = total[s * half:(s + 1) * half].reshape(8 * half, B)
        flat[s, 8 * half:8 * half + 4] = total[2 * half, 4 * s:4 * s + 4]
        flat[s, 8 * half + 4:] = jnp.zeros((flat.shape[1] - 8 * half - 4, B), f32)
    for t in range(out.shape[0]):
        for s in range(2):
            out[t, 3 * s:3 * s + 3] = flat[s, 3 * t:3 * t + 3]
            out[t, 6 + s:7 + s] = jnp.full((1, B), decay_ref[s], f32)


def scan_kernel(chunks, out):
    now = jnp.zeros((3, B), f32)
    for t in range(chunks.shape[0]):
        for s in range(2):
            now = chunks[t, 6 + s:7 + s] * now + chunks[t, 3 * s:3 * s + 3]
            out[s, t, 0:3] = now
            out[s, t, 3:4] = jnp.zeros((1, B), f32)


def unpack_kernel(chunks, out, flat):
    half = (out.shape[0] - 1) // 2
    for g in range(2):
        for t in range(chunks.shape[1]):
            flat[g, 3 * t:3 * t + 3] = chunks[g, t, 0:3]
        out[g * half:(g + 1) * half] = flat[g, 0:8 * half].reshape(half, 8, B)
        out[2 * half, 4 * g:4 * g + 4] = flat[g, 8 * half:8 * half + 4]


def spread(row):
    return jnp.broadcast_to(row, (8, B))


def invert_factor(rows, lane, sub):
    groups = len(rows)
    for j in range(groups):
        o = 8 * j
        top = rows[j]
        inside = (lane >= o) & (lane < o + 8)
        cols = [jnp.broadcast_to(top[:, o + m:o + m + 1], (8, B)) for m in range(8)]
        a = {(r, m): spread(cols[m][r:r + 1]) for m in range(8) for r in range(m, 8)}
        d = []
        for m in range(8):
            unit = jnp.where(lane == o + m, 1.0, 0.0)
            d.append(jnp.where(inside, unit, spread(top[m:m + 1])))
        low, rs, u = {}, [], []
        for k in range(8):
            r = lax.rsqrt(a[k, k])
            rs.append(r)
            for m in range(k + 1, 8):
                low[m, k] = a[m, k] * r
            for m in range(k + 1, 8):
                for n in range(m, 8):
                    a[n, m] = a[n, m] - low[n, k] * low[m, k]
            u.append(d[k] * r)
            for m in range(k + 1, 8):
                d[m] = d[m] - low[m, k] * u[k]
        w = [None] * 8
        for m in range(7, -1, -1):
            acc = u[m]
            for k in range(7, m, -1):
                acc = acc - low[k, m] * w[k]
            w[m] = acc * rs[m]
        for i in range(j + 1, groups):
            old = rows[i]
            new = jnp.where(inside, 0.0, old)
            for m in range(7, -1, -1):
                new = new - jnp.broadcast_to(old[:, o + m:o + m + 1], (8, B)) * w[m]
            rows[i] = new
        merged = u[0]
        for m in range(1, 8):
            merged = jnp.where(sub == m, u[m], merged)
        rows[j] = merged
    return rows


def solve_kernel(z_ref, pieces, keep, send, mat, upper, inv, vec, sol):
    z = z_ref[0]
    width = mat.shape[0]
    nb = width // B
    blocks = block_list(nb)
    nblk = len(blocks)
    lane = lax.broadcasted_iota(jnp.int32, (8, B), 1)
    sub = lax.broadcasted_iota(jnp.int32, (8, B), 0)
    row_i = lax.broadcasted_iota(jnp.int32, (B, B), 0)
    col_i = lax.broadcasted_iota(jnp.int32, (B, B), 1)
    row_w = lax.broadcasted_iota(jnp.int32, (B, width), 0)
    col_w = lax.broadcasted_iota(jnp.int32, (B, width), 1)
    vec[...] = jnp.zeros(vec.shape, f32)
    for i, (b, c) in enumerate(blocks):
        if c > b:
            mat[c * B:(c + 1) * B, b * B:(b + 1) * B] = jnp.zeros((B, B), f32)
        for h in range(pieces.shape[0]):
            for g in range(2):
                at = b * B + (2 * h + g) * 8
                mat[at:at + 8, c * B:(c + 1) * B] = pieces[h, g * nblk + i]
    for b in range(nb):
        vec[0:1, b * B:(b + 1) * B] = pieces[0, 2 * nblk, b:b + 1]

    def step(b, carry):
        at = pl.multiple_of(b * B, B)
        diag = mat[pl.ds(at, B), pl.ds(at, B)]
        rows = invert_factor([diag[8 * i:8 * i + 8] for i in range(B // 8)], lane, sub)
        left = jnp.where(col_i <= row_i, jnp.concatenate(rows, axis=0), 0.0)
        inv[b] = left
        panel = jnp.dot(left, mat[pl.ds(at, B), :], precision=HIGH, preferred_element_type=f32)
        panel = jnp.where(col_w >= row_w + at, panel, 0.0)
        upper[pl.ds(at, B), :] = panel
        y = lax.dot_general(vec[:, pl.ds(at, B)], left, (((1,), (1,)), ((), ())),
                            precision=HIGH, preferred_element_type=f32)
        sol[:, pl.ds(at, B)] = y
        vec[...] = vec[...] - jnp.dot(y, panel, precision=HIGH, preferred_element_type=f32)
        mat[...] = mat[...] - lax.dot_general(panel, panel, (((0,), (0,)), ((), ())),
                                              precision=HIGH, preferred_element_type=f32)
        return carry

    lax.fori_loop(0, nb, step, 0)

    vec[...] = jnp.zeros(vec.shape, f32)
    for b in range(nb - 1, -1, -1):
        y = sol[:, b * B:(b + 1) * B]
        if b < nb - 1:
            y = y - lax.dot_general(
                vec[:, (b + 1) * B:], upper[b * B:(b + 1) * B, (b + 1) * B:],
                (((1,), (1,)), ((), ())), precision=HIGH, preferred_element_type=f32)
        vec[:, b * B:(b + 1) * B] = jnp.dot(y, inv[b], precision=HIGH, preferred_element_type=f32)
    share = keep.shape[0] - 8
    other = z + 1 - 2 * lax.rem(z, 2)
    keep[0:share] = upper[pl.ds(pl.multiple_of(z * share, share), share), :]
    send[0:share] = upper[pl.ds(pl.multiple_of(other * share, share), share), :]
    keep[share:] = vec[...]
    send[share:] = vec[...]


def join_kernel(z_ref, keep, got, factor, state):
    share = factor.shape[1]
    s = lax.rem(z_ref[0], 2)
    factor[s] = keep[0:share]
    factor[1 - s] = got[0:share]
    first = jnp.where(s == 0, keep[share:share + 1], got[share:share + 1])
    second = jnp.where(s == 0, got[share:share + 1], keep[share:share + 1])
    state[0:1] = first
    state[1:2] = second


def shifted(value, by):
    count = lax.axis_size(ROWS)
    return lax.ppermute(value, ROWS, [(i, (i + by) % count) for i in range(count)])


def on_device(jacobian, rhs, forget, restart):
    segs, rows, width = jacobian.shape
    nb = width // B
    tiles = segs * len(block_list(nb)) + 1
    tms = lax.axis_size("tm")
    z = lax.axis_index(ROWS)
    z_now = z.astype(jnp.int32).reshape(1)
    share = width // lax.axis_size(ROWS)
    decays = forget * (1.0 - 0.2 * restart.astype(f32))

    four, two, one = tile_array(4, tiles), tile_array(2, tiles), tile_array(tiles)
    own, up, down, up2, down2 = pl.pallas_call(
        pack_kernel, out_shape=[four, four, four, two, two],
        in_specs=[SM, VM, VM], out_specs=[VM] * 5,
        scratch_shapes=[pltpu.VMEM((4, 4, tiles, 8, B), f32)],
        compiler_params=PARAMS, name="pack")(z_now, jacobian, rhs)
    up, down, up2, down2 = shifted(up, 1), shifted(down, -1), shifted(up2, 2), shifted(down2, -2)
    mine, plus, minus, far = pl.pallas_call(
        first_sum_kernel, out_shape=[one] * 4,
        in_specs=[SM] + [VM] * 5, out_specs=[VM] * 4,
        scratch_shapes=[pltpu.VMEM((4, tiles, 8, B), f32)],
        compiler_params=PARAMS, name="first_sum")(z_now, own, up, down, up2, down2)
    plus, minus, far = shifted(plus, 4), shifted(minus, -4), shifted(far, 8)
    chunks = pl.pallas_call(
        second_sum_kernel, out_shape=tile_array(tms),
        in_specs=[SM] + [VM] * 4, out_specs=VM,
        scratch_shapes=[pltpu.VMEM((2, 3 * tms, B), f32)],
        compiler_params=PARAMS, name="second_sum")(decays, mine, plus, minus, far)
    chunks = lax.all_to_all(chunks, "tm", 0, 0)
    chunks = pl.pallas_call(
        scan_kernel, out_shape=jax.ShapeDtypeStruct((2, tms, 4, B), f32), in_specs=[VM], out_specs=VM,
        compiler_params=PARAMS, name="scan")(chunks)
    chunks = lax.all_to_all(chunks.reshape(2 * tms, 4, B), ("side", "tm"), 0, 0)
    mine = pl.pallas_call(
        unpack_kernel, out_shape=one, in_specs=[VM], out_specs=VM,
        scratch_shapes=[pltpu.VMEM((2, 3 * tms, B), f32)],
        compiler_params=PARAMS, name="unpack")(chunks.reshape(2, tms, 4, B))
    pieces = lax.all_gather(mine, "pair")
    keep, send = pl.pallas_call(
        solve_kernel,
        out_shape=[jax.ShapeDtypeStruct((share + 8, width), f32)] * 2,
        in_specs=[SM, VM], out_specs=[VM] * 2,
        scratch_shapes=[
            pltpu.VMEM((width, width), f32), pltpu.VMEM((width, width), f32),
            pltpu.VMEM((nb, B, B), f32), pltpu.VMEM((8, width), f32), pltpu.VMEM((8, width), f32)],
        compiler_params=PARAMS, name="solve")(z_now, pieces)
    got = lax.ppermute(send, "side", [(0, 1), (1, 0)])
    factor, state = pl.pallas_call(
        join_kernel,
        out_shape=[jax.ShapeDtypeStruct((segs, share, width), f32), jax.ShapeDtypeStruct((segs, width), f32)],
        in_specs=[SM, VM, VM], out_specs=[VM] * 2,
        compiler_params=PARAMS, name="join")(z_now, keep, got)
    return (factor, lax.dynamic_slice_in_dim(state, z * share, share, 1))


def solution(mesh):
    count, tms = mesh.devices.shape
    paired = Mesh(mesh.devices.reshape(count // 2, 2, tms), ("pair", "side", "tm"))
    in_specs = (P("tm", ROWS, None), P("tm", ROWS), P("tm"), P("tm"))
    out_specs = (P("tm", ROWS, None), P("tm", ROWS))
    return jax.shard_map(
        on_device, mesh=paired, in_specs=in_specs, out_specs=out_specs, check_vma=False
    )
```

```python
import functools
import jax
import jax.numpy as jnp
from jax import lax
from jax.experimental import pallas as pl
from jax.experimental.pallas import tpu as pltpu
from jax.sharding import Mesh, PartitionSpec as P

f32 = jnp.float32
B = 128
ROWS = ("pair", "side")
HIGH = lax.Precision.HIGHEST
VM = pl.BlockSpec(memory_space=pltpu.VMEM)
SM = pl.BlockSpec(memory_space=pltpu.SMEM)
PARAMS = pltpu.CompilerParams(vmem_limit_bytes=48 << 20)


def block_list(nb):
    return [(b, c) for b in range(nb) for c in range(b, nb)]


def tile_array(*lead):
    return jax.ShapeDtypeStruct(tuple(lead) + (8, B), f32)


def pack_kernel(z_ref, jac_ref, rhs_ref, own, up, down, up2, down2, parts):
    z = z_ref[0]
    segs, rows, width = jac_ref.shape
    nb = width // B
    blocks = block_list(nb)
    last = segs * len(blocks)
    for p in range(4):
        for a in range(4):
            parts[p, a, last] = jnp.zeros((8, B), f32)
    grads = []
    for s in range(segs):
        jac = jac_ref[s]
        for b in range(nb):
            info = lax.dot_general(
                jac[:, b * B:(b + 1) * B], jac[:, b * B:],
                (((0,), (0,)), ((), ())), preferred_element_type=f32)
            for c in range(b, nb):
                tile = s * len(blocks) + blocks.index((b, c))
                piece = info[:, (c - b) * B:(c - b + 1) * B].reshape(4, 4, 8, B)
                for q in range(4):
                    p = lax.rem(q + 16 - z, 4)
                    for a in range(4):
                        parts[p, a, tile] = piece[a, q]
        grads.append(jnp.dot(rhs_ref[...], jac, preferred_element_type=f32)[s:s + 1])
    p = lax.rem(16 - z, 4)
    for s in range(segs):
        for b in range(nb):
            parts[p, 0, last, pl.ds(s * nb + b, 1), :] = grads[s][:, b * B:(b + 1) * B]
    own[...] = parts[0]
    up[...] = parts[1]
    up2[...] = parts[2, 0:2]
    down2[...] = parts[2, 2:4]
    down[...] = parts[3]


def first_sum_kernel(z_ref, own, up, down, up2, down2, mine, plus, minus, far, total):
    h = lax.div(z_ref[0], 4)
    near = own[...] + up[...] + down[...]
    total[0:2] = near[0:2] + up2[...]
    total[2:4] = near[2:4] + down2[...]
    mine[...] = total[h]
    plus[...] = total[lax.rem(h + 1, 4)]
    minus[...] = total[lax.rem(h + 3, 4)]
    far[...] = total[lax.rem(h + 2, 4)]


def second_sum_kernel(decay_ref, mine, plus, minus, far, out, flat):
    total = (mine[...] + plus[...]) + (minus[...] + far[...])
    half = (total.shape[0] - 1) // 2
    for s in range(2):
        flat[s, 0:8 * half] = total[s * half:(s + 1) * half].reshape(8 * half, B)
        flat[s, 8 * half:8 * half + 4] = total[2 * half, 4 * s:4 * s + 4]
        flat[s, 8 * half + 4:] = jnp.zeros((flat.shape[1] - 8 * half - 4, B), f32)
    for t in range(out.shape[0]):
        for s in range(2):
            out[t, 3 * s:3 * s + 3] = flat[s, 3 * t:3 * t + 3]
            out[t, 6 + s:7 + s] = jnp.full((1, B), decay_ref[s], f32)


def scan_kernel(chunks, out):
    now = jnp.zeros((3, B), f32)
    for t in range(chunks.shape[0]):
        for s in range(2):
            now = chunks[t, 6 + s:7 + s] * now + chunks[t, 3 * s:3 * s + 3]
            out[s, t, 0:3] = now
            out[s, t, 3:4] = jnp.zeros((1, B), f32)


def unpack_kernel(chunks, out, flat):
    half = (out.shape[0] - 1) // 2
    for g in range(2):
        for t in range(chunks.shape[1]):
            flat[g, 3 * t:3 * t + 3] = chunks[g, t, 0:3]
        out[g * half:(g + 1) * half] = flat[g, 0:8 * half].reshape(half, 8, B)
        out[2 * half, 4 * g:4 * g + 4] = flat[g, 8 * half:8 * half + 4]


def spread(row):
    return jnp.broadcast_to(row, (8, B))


def across(value, lane):
    return jnp.broadcast_to(value[:, lane:lane + 1], (8, B))


def invert_factor(rows, lane, sub, jobs):
    groups = len(rows)
    jobs = list(jobs)
    cols = [across(rows[0], m) for m in range(8)]
    for j in range(groups):
        o = 8 * j
        top = rows[j]
        more = j + 1 < groups
        inside = (lane >= o) & (lane < o + 8)
        a = {(r, m): spread(cols[m][r:r + 1]) for m in range(8) for r in range(m, 8)}
        if more:
            left = [across(rows[j + 1], o + m) for m in range(8)]
            cols = [across(rows[j + 1], o + 8 + m) for m in range(8)]
            after = jnp.where(inside, 0.0, rows[j + 1])
        d = []
        for m in range(8):
            unit = jnp.where(lane == o + m, 1.0, 0.0)
            d.append(jnp.where(inside, unit, spread(top[m:m + 1])))
        low, rs, u = {}, [], []
        for k in range(8):
            r = lax.rsqrt(a[k, k])
            rs.append(r)
            for m in range(k + 1, 8):
                low[m, k] = a[m, k] * r
            for m in range(k + 1, 8):
                for n in range(m, 8):
                    a[n, m] = a[n, m] - low[n, k] * low[m, k]
            u.append(d[k] * r)
            for m in range(k + 1, 8):
                d[m] = d[m] - low[m, k] * u[k]
            if more:
                col = left[k] * r
                for m in range(k + 1, 8):
                    left[m] = left[m] - col * low[m, k]
                for m in range(8):
                    cols[m] = cols[m] - col * spread(col[m:m + 1])
                after = after - col * u[k]
        if more:
            rows[j + 1] = after
        w = [None] * 8
        for m in range(7, -1, -1):
            acc = u[m]
            for k in range(7, m, -1):
                acc = acc - low[k, m] * w[k]
            w[m] = acc * rs[m]
        for i in range(j + 2, groups):
            old = rows[i]
            new = jnp.where(inside, 0.0, old)
            for m in range(7, -1, -1):
                new = new - across(old, o + m) * w[m]
            rows[i] = new
        merged = u[0]
        for m in range(1, 8):
            merged = jnp.where(sub == m, u[m], merged)
        rows[j] = merged
        if jobs:
            jobs.pop(0)()
    for job in jobs:
        job()
    return rows


def times(x, y):
    return jnp.dot(x, y, precision=HIGH, preferred_element_type=f32)


def left_transposed(x, y):
    return lax.dot_general(x, y, (((0,), (0,)), ((), ())), precision=HIGH, preferred_element_type=f32)


def right_transposed(x, y):
    return lax.dot_general(x, y, (((1,), (1,)), ((), ())), precision=HIGH, preferred_element_type=f32)


def solve_kernel(z_ref, pieces, keep, send, mat, upper, inv, vec, sol):
    z = z_ref[0]
    width = mat.shape[0]
    nb = width // B
    blocks = block_list(nb)
    nblk = len(blocks)
    lane = lax.broadcasted_iota(jnp.int32, (8, B), 1)
    sub = lax.broadcasted_iota(jnp.int32, (8, B), 0)
    row_i = lax.broadcasted_iota(jnp.int32, (B, B), 0)
    col_i = lax.broadcasted_iota(jnp.int32, (B, B), 1)
    vec[...] = jnp.zeros(vec.shape, f32)
    for i, (b, c) in enumerate(blocks):
        for h in range(pieces.shape[0]):
            for g in range(2):
                at = b * B + (2 * h + g) * 8
                mat[at:at + 8, c * B:(c + 1) * B] = pieces[h, g * nblk + i]
    for b in range(nb):
        vec[0:1, b * B:(b + 1) * B] = pieces[0, 2 * nblk, b:b + 1]

    def span(b):
        return slice(b * B, (b + 1) * B)

    def panel(b, c):
        upper[span(b), span(c)] = times(inv[b], mat[span(b), span(c)])

    def diagonal(b):
        block = times(inv[b], mat[span(b), span(b)])
        upper[span(b), span(b)] = jnp.where(col_i >= row_i, block, 0.0)
        if b:
            upper[span(b), 0:b * B] = jnp.zeros((B, b * B), f32)

    def trail(b, c, d):
        mat[span(c), span(d)] = mat[span(c), span(d)] - left_transposed(upper[span(b), span(c)], upper[span(b), span(d)])

    def forward(b):
        sol[:, span(b)] = right_transposed(vec[:, span(b)], inv[b])

    def advance(b, c):
        vec[:, span(c)] = vec[:, span(c)] - times(sol[:, span(b)], upper[span(b), span(c)])

    jobs = []
    for b in range(nb):
        rows = [mat[b * B + 8 * i:b * B + 8 * i + 8, span(b)] for i in range(B // 8)]
        rows = invert_factor(rows, lane, sub, jobs)
        inv[b] = jnp.where(col_i <= row_i, jnp.concatenate(rows, axis=0), 0.0)
        jobs = []
        if b + 1 < nb:
            panel(b, b + 1)
            trail(b, b + 1, b + 1)
        for c in range(b + 2, nb):
            jobs.append(functools.partial(panel, b, c))
        for c in range(b + 1, nb):
            for d in range(c, nb):
                if d > b + 1:
                    jobs.append(functools.partial(trail, b, c, d))
        jobs.append(functools.partial(diagonal, b))
        jobs.append(functools.partial(forward, b))
        for c in range(b + 1, nb):
            jobs.append(functools.partial(advance, b, c))
    for job in jobs:
        job()

    for b in range(nb - 1, -1, -1):
        y = sol[:, span(b)]
        if b + 1 < nb:
            y = y - right_transposed(vec[:, (b + 1) * B:], upper[span(b), (b + 1) * B:])
        vec[:, span(b)] = times(y, inv[b])
    share = keep.shape[0] - 8
    other = z + 1 - 2 * lax.rem(z, 2)
    keep[0:share] = upper[pl.ds(pl.multiple_of(z * share, share), share), :]
    send[0:share] = upper[pl.ds(pl.multiple_of(other * share, share), share), :]
    keep[share:] = vec[...]
    send[share:] = vec[...]


def join_kernel(z_ref, keep, got, factor, state):
    share = factor.shape[1]
    s = lax.rem(z_ref[0], 2)
    factor[s] = keep[0:share]
    factor[1 - s] = got[0:share]
    first = jnp.where(s == 0, keep[share:], got[share:])
    second = jnp.where(s == 0, got[share:], keep[share:])
    left = first.shape[1] - z_ref[0] * share
    state[0:1] = pltpu.roll(first, left, 1)[0:1, 0:share]
    state[1:2] = pltpu.roll(second, left, 1)[0:1, 0:share]


def shifted(value, by):
    count = lax.axis_size(ROWS)
    return lax.ppermute(value, ROWS, [(i, (i + by) % count) for i in range(count)])


def on_device(jacobian, rhs, forget, restart):
    segs, rows, width = jacobian.shape
    nb = width // B
    tiles = segs * len(block_list(nb)) + 1
    tms = lax.axis_size("tm")
    z = lax.axis_index(ROWS)
    z_now = z.astype(jnp.int32).reshape(1)
    share = width // lax.axis_size(ROWS)
    decays = forget * (1.0 - 0.2 * restart.astype(f32))

    four, two, one = tile_array(4, tiles), tile_array(2, tiles), tile_array(tiles)
    own, up, down, up2, down2 = pl.pallas_call(
        pack_kernel, out_shape=[four, four, four, two, two],
        in_specs=[SM, VM, VM], out_specs=[VM] * 5,
        scratch_shapes=[pltpu.VMEM((4, 4, tiles, 8, B), f32)],
        compiler_params=PARAMS, name="pack")(z_now, jacobian, rhs)
    up, down, up2, down2 = shifted(up, 1), shifted(down, -1), shifted(up2, 2), shifted(down2, -2)
    mine, plus, minus, far = pl.pallas_call(
        first_sum_kernel, out_shape=[one] * 4,
        in_specs=[SM] + [VM] * 5, out_specs=[VM] * 4,
        scratch_shapes=[pltpu.VMEM((4, tiles, 8, B), f32)],
        compiler_params=PARAMS, name="first_sum")(z_now, own, up, down, up2, down2)
    plus, minus, far = shifted(plus, 4), shifted(minus, -4), shifted(far, 8)
    chunks = pl.pallas_call(
        second_sum_kernel, out_shape=tile_array(tms),
        in_specs=[SM] + [VM] * 4, out_specs=VM,
        scratch_shapes=[pltpu.VMEM((2, 3 * tms, B), f32)],
        compiler_params=PARAMS, name="second_sum")(decays, mine, plus, minus, far)
    chunks = lax.all_to_all(chunks, "tm", 0, 0)
    chunks = pl.pallas_call(
        scan_kernel, out_shape=jax.ShapeDtypeStruct((2, tms, 4, B), f32), in_specs=[VM], out_specs=VM,
        compiler_params=PARAMS, name="scan")(chunks)
    chunks = lax.all_to_all(chunks.reshape(2 * tms, 4, B), ("side", "tm"), 0, 0)
    mine = pl.pallas_call(
        unpack_kernel, out_shape=one, in_specs=[VM], out_specs=VM,
        scratch_shapes=[pltpu.VMEM((2, 3 * tms, B), f32)],
        compiler_params=PARAMS, name="unpack")(chunks.reshape(2, tms, 4, B))
    pieces = lax.all_gather(mine, "pair")
    keep, send = pl.pallas_call(
        solve_kernel,
        out_shape=[jax.ShapeDtypeStruct((share + 8, width), f32)] * 2,
        in_specs=[SM, VM], out_specs=[VM] * 2,
        scratch_shapes=[
            pltpu.VMEM((width, width), f32), pltpu.VMEM((width, width), f32),
            pltpu.VMEM((nb, B, B), f32), pltpu.VMEM((8, width), f32), pltpu.VMEM((8, width), f32)],
        compiler_params=PARAMS, name="solve")(z_now, pieces)
    got = lax.ppermute(send, "side", [(0, 1), (1, 0)])
    factor, state = pl.pallas_call(
        join_kernel,
        out_shape=[jax.ShapeDtypeStruct((segs, share, width), f32), jax.ShapeDtypeStruct((segs, share), f32)],
        in_specs=[SM, VM, VM], out_specs=[VM] * 2,
        compiler_params=PARAMS, name="join")(z_now, keep, got)
    return (factor, state)


def solution(mesh):
    count, tms = mesh.devices.shape
    paired = Mesh(mesh.devices.reshape(count // 2, 2, tms), ("pair", "side", "tm"))
    in_specs = (P("tm", ROWS, None), P("tm", ROWS), P("tm"), P("tm"))
    out_specs = (P("tm", ROWS, None), P("tm", ROWS))
    return jax.shard_map(
        on_device, mesh=paired, in_specs=in_specs, out_specs=out_specs, check_vma=False
    )
```

```python
import functools
import jax
import jax.numpy as jnp
from jax import lax
from jax.experimental import pallas as pl
from jax.experimental.pallas import tpu as pltpu
from jax.sharding import Mesh, PartitionSpec as P

f32 = jnp.float32
B = 128
ROWS = ("half", "quarter", "near", "side")
HIGH = lax.Precision.HIGHEST
VM = pl.BlockSpec(memory_space=pltpu.VMEM)
SM = pl.BlockSpec(memory_space=pltpu.SMEM)
PARAMS = pltpu.CompilerParams(vmem_limit_bytes=48 << 20)


def block_list(nb):
    return [(b, c) for b in range(nb) for c in range(b, nb) if b < nb - 1]


def tile_array(*lead):
    return jax.ShapeDtypeStruct(tuple(lead) + (8, B), f32)


def spare_quarter():
    row = lax.broadcasted_iota(jnp.int32, (B, B), 0)
    col = lax.broadcasted_iota(jnp.int32, (B, B), 1)
    return (row >= B // 2) & (col < B // 2)


def swap_halves(block):
    return jnp.concatenate([block[B // 2:], block[:B // 2]], axis=0)


def pack_kernel(z_ref, jac_ref, rhs_ref, own, up, down, up2, down2, parts):
    z = z_ref[0]
    segs, rows, width = jac_ref.shape
    nb = width // B
    blocks = block_list(nb)
    last = segs * len(blocks)
    for p in range(4):
        for a in range(4):
            parts[p, a, last] = jnp.zeros((8, B), f32)
    grads = []
    spare = spare_quarter()
    for s in range(segs):
        jac = jac_ref[s]
        quarters = None
        for b in range(nb - 1, -1, -1):
            info = lax.dot_general(
                jac[:, b * B:(b + 1) * B], jac[:, b * B:],
                (((0,), (0,)), ((), ())), preferred_element_type=f32)
            if b == nb - 1:
                turned = pltpu.roll(info, B // 2, 1)
                quarters = [swap_halves(info), swap_halves(turned), turned]
                continue
            for c in range(b, nb):
                tile = s * len(blocks) + blocks.index((b, c))
                block = info[:, (c - b) * B:(c - b + 1) * B]
                if c == b:
                    block = jnp.where(spare, quarters[b], block)
                piece = block.reshape(4, 4, 8, B)
                for q in range(4):
                    p = lax.rem(q + 16 - z, 4)
                    for a in range(4):
                        parts[p, a, tile] = piece[a, q]
        grads.append(jnp.dot(rhs_ref[...], jac, preferred_element_type=f32)[s:s + 1])
    p = lax.rem(16 - z, 4)
    for s in range(segs):
        for b in range(nb):
            parts[p, 0, last, pl.ds(s * nb + b, 1), :] = grads[s][:, b * B:(b + 1) * B]
    own[...] = parts[0]
    up[...] = parts[1]
    up2[...] = parts[2, 0:2]
    down2[...] = parts[2, 2:4]
    down[...] = parts[3]


def first_sum_kernel(z_ref, own, up, down, up2, down2, mine, plus, minus, far, total):
    h = lax.div(z_ref[0], 4)
    near = own[...] + up[...] + down[...]
    total[0:2] = near[0:2] + up2[...]
    total[2:4] = near[2:4] + down2[...]
    mine[...] = total[h]
    plus[...] = total[lax.rem(h + 1, 4)]
    minus[...] = total[lax.rem(h + 3, 4)]
    far[...] = total[lax.rem(h + 2, 4)]


def second_sum_kernel(z_ref, decay_ref, mine, plus, minus, far, out, flat):
    total = (mine[...] + plus[...]) + (minus[...] + far[1 - lax.div(z_ref[0], 8)])
    half = (total.shape[0] - 1) // 2
    for s in range(2):
        flat[s, 0:8 * half] = total[s * half:(s + 1) * half].reshape(8 * half, B)
        flat[s, 8 * half:8 * half + 4] = total[2 * half, 4 * s:4 * s + 4]
        flat[s, 8 * half + 4:] = jnp.zeros((flat.shape[1] - 8 * half - 4, B), f32)
    for t in range(out.shape[0]):
        for s in range(2):
            out[t, 3 * s:3 * s + 3] = flat[s, 3 * t:3 * t + 3]
            out[t, 6 + s:7 + s] = jnp.full((1, B), decay_ref[s], f32)


def scan_kernel(chunks, out):
    now = jnp.zeros((3, B), f32)
    for t in range(chunks.shape[0]):
        for s in range(2):
            now = chunks[t, 6 + s:7 + s] * now + chunks[t, 3 * s:3 * s + 3]
            out[s, t, 0:3] = now
            out[s, t, 3:4] = jnp.zeros((1, B), f32)


def unpack_kernel(chunks, out, flat):
    half = (out.shape[0] - 1) // 2
    for g in range(2):
        for t in range(chunks.shape[1]):
            flat[g, 3 * t:3 * t + 3] = chunks[g, t, 0:3]
        out[g * half:(g + 1) * half] = flat[g, 0:8 * half].reshape(half, 8, B)
        out[2 * half, 4 * g:4 * g + 4] = flat[g, 8 * half:8 * half + 4]


def spread(row):
    return jnp.broadcast_to(row, (8, B))


def across(value, lane):
    return jnp.broadcast_to(value[:, lane:lane + 1], (8, B))


def invert_factor(rows, lane, sub, jobs):
    groups = len(rows)
    jobs = list(jobs)
    cols = [across(rows[0], m) for m in range(8)]
    for j in range(groups):
        o = 8 * j
        top = rows[j]
        more = j + 1 < groups
        inside = (lane >= o) & (lane < o + 8)
        a = {(r, m): spread(cols[m][r:r + 1]) for m in range(8) for r in range(m, 8)}
        if more:
            left = [across(rows[j + 1], o + m) for m in range(8)]
            cols = [across(rows[j + 1], o + 8 + m) for m in range(8)]
            after = jnp.where(inside, 0.0, rows[j + 1])
        d = []
        for m in range(8):
            unit = jnp.where(lane == o + m, 1.0, 0.0)
            d.append(jnp.where(inside, unit, spread(top[m:m + 1])))
        low, rs, u = {}, [], []
        for k in range(8):
            r = lax.rsqrt(a[k, k])
            rs.append(r)
            for m in range(k + 1, 8):
                low[m, k] = a[m, k] * r
            for m in range(k + 1, 8):
                for n in range(m, 8):
                    a[n, m] = a[n, m] - low[n, k] * low[m, k]
            u.append(d[k] * r)
            for m in range(k + 1, 8):
                d[m] = d[m] - low[m, k] * u[k]
            if more:
                col = left[k] * r
                for m in range(k + 1, 8):
                    left[m] = left[m] - col * low[m, k]
                for m in range(8):
                    cols[m] = cols[m] - col * spread(col[m:m + 1])
                after = after - col * u[k]
        if more:
            rows[j + 1] = after
        w = [None] * 8
        for m in range(7, -1, -1):
            acc = u[m]
            for k in range(7, m, -1):
                acc = acc - low[k, m] * w[k]
            w[m] = acc * rs[m]
        for i in range(j + 2, groups):
            old = rows[i]
            new = jnp.where(inside, 0.0, old)
            for m in range(7, -1, -1):
                new = new - across(old, o + m) * w[m]
            rows[i] = new
        merged = u[0]
        for m in range(1, 8):
            merged = jnp.where(sub == m, u[m], merged)
        rows[j] = merged
        if jobs:
            jobs.pop(0)()
    for job in jobs:
        job()
    return rows


def times(x, y):
    return jnp.dot(x, y, precision=HIGH, preferred_element_type=f32)


def left_transposed(x, y):
    return lax.dot_general(x, y, (((0,), (0,)), ((), ())), precision=HIGH, preferred_element_type=f32)


def right_transposed(x, y):
    return lax.dot_general(x, y, (((1,), (1,)), ((), ())), precision=HIGH, preferred_element_type=f32)


def solve_kernel(z_ref, pieces, keep, send, mat, upper, inv, vec, sol):
    z = z_ref[0]
    width = mat.shape[0]
    nb = width // B
    blocks = block_list(nb)
    nblk = len(blocks)
    lane = lax.broadcasted_iota(jnp.int32, (8, B), 1)
    sub = lax.broadcasted_iota(jnp.int32, (8, B), 0)
    row_i = lax.broadcasted_iota(jnp.int32, (B, B), 0)
    col_i = lax.broadcasted_iota(jnp.int32, (B, B), 1)
    vec[...] = jnp.zeros(vec.shape, f32)
    for i, (b, c) in enumerate(blocks):
        for h in range(pieces.shape[0]):
            for g in range(2):
                at = b * B + (2 * h + g) * 8
                mat[at:at + 8, c * B:(c + 1) * B] = pieces[h, g * nblk + i]
    for b in range(nb):
        vec[0:1, b * B:(b + 1) * B] = pieces[0, 2 * nblk, b:b + 1]

    def span(b):
        return slice(b * B, (b + 1) * B)

    def panel(b, c):
        upper[span(b), span(c)] = times(inv[b], mat[span(b), span(c)])

    def diagonal(b):
        block = times(inv[b], mat[span(b), span(b)])
        upper[span(b), span(b)] = jnp.where(col_i >= row_i, block, 0.0)
        if b:
            upper[span(b), 0:b * B] = jnp.zeros((B, b * B), f32)

    def trail(b, c, d):
        mat[span(c), span(d)] = mat[span(c), span(d)] - left_transposed(upper[span(b), span(c)], upper[span(b), span(d)])

    def forward(b):
        sol[:, span(b)] = right_transposed(vec[:, span(b)], inv[b])

    def advance(b, c):
        vec[:, span(c)] = vec[:, span(c)] - times(sol[:, span(b)], upper[span(b), span(c)])

    spare = spare_quarter()
    first, second, third = [mat[span(b), span(b)] for b in range(3)]
    right = col_i >= B // 2
    mat[span(3), span(3)] = jnp.where(
        row_i < B // 2,
        jnp.where(right, pltpu.roll(swap_halves(second), B // 2, 1), swap_halves(first)),
        pltpu.roll(third, B // 2, 1))

    def mirror(b):
        block = mat[span(b), span(b)]
        mat[span(b), span(b)] = jnp.where(spare, block.T, block)

    mirror(0)
    jobs = [functools.partial(mirror, b) for b in range(1, nb)]
    for b in range(nb):
        rows = [mat[b * B + 8 * i:b * B + 8 * i + 8, span(b)] for i in range(B // 8)]
        rows = invert_factor(rows, lane, sub, jobs)
        inv[b] = jnp.where(col_i <= row_i, jnp.concatenate(rows, axis=0), 0.0)
        jobs = []
        if b + 1 < nb:
            panel(b, b + 1)
            trail(b, b + 1, b + 1)
        for c in range(b + 2, nb):
            jobs.append(functools.partial(panel, b, c))
        for c in range(b + 1, nb):
            for d in range(c, nb):
                if d > b + 1:
                    jobs.append(functools.partial(trail, b, c, d))
        jobs.append(functools.partial(diagonal, b))
        jobs.append(functools.partial(forward, b))
        for c in range(b + 1, nb):
            jobs.append(functools.partial(advance, b, c))
    for job in jobs:
        job()

    for b in range(nb - 1, -1, -1):
        y = sol[:, span(b)]
        if b + 1 < nb:
            y = y - right_transposed(vec[:, (b + 1) * B:], upper[span(b), (b + 1) * B:])
        vec[:, span(b)] = times(y, inv[b])
    share = keep.shape[0] - 8
    other = z + 1 - 2 * lax.rem(z, 2)
    keep[0:share] = upper[pl.ds(pl.multiple_of(z * share, share), share), :]
    send[0:share] = upper[pl.ds(pl.multiple_of(other * share, share), share), :]
    keep[share:] = vec[...]
    send[share:] = vec[...]


def join_kernel(z_ref, keep, got, factor, state):
    share = factor.shape[1]
    s = lax.rem(z_ref[0], 2)
    factor[s] = keep[0:share]
    factor[1 - s] = got[0:share]
    first = jnp.where(s == 0, keep[share:], got[share:])
    second = jnp.where(s == 0, got[share:], keep[share:])
    left = first.shape[1] - z_ref[0] * share
    state[0:1] = pltpu.roll(first, left, 1)[0:1, 0:share]
    state[1:2] = pltpu.roll(second, left, 1)[0:1, 0:share]


def shifted(value, by):
    count = lax.axis_size(ROWS)
    return lax.ppermute(value, ROWS, [(i, (i + by) % count) for i in range(count)])


def on_device(jacobian, rhs, forget, restart):
    segs, rows, width = jacobian.shape
    nb = width // B
    tiles = segs * len(block_list(nb)) + 1
    tms = lax.axis_size("tm")
    z = lax.axis_index(ROWS)
    z_now = z.astype(jnp.int32).reshape(1)
    share = width // lax.axis_size(ROWS)
    decays = forget * (1.0 - 0.2 * restart.astype(f32))

    four, two, one = tile_array(4, tiles), tile_array(2, tiles), tile_array(tiles)
    own, up, down, up2, down2 = pl.pallas_call(
        pack_kernel, out_shape=[four, four, four, two, two],
        in_specs=[SM, VM, VM], out_specs=[VM] * 5,
        scratch_shapes=[pltpu.VMEM((4, 4, tiles, 8, B), f32)],
        compiler_params=PARAMS, name="pack")(z_now, jacobian, rhs)
    up, down, up2, down2 = shifted(up, 1), shifted(down, -1), shifted(up2, 2), shifted(down2, -2)
    mine, plus, minus, far = pl.pallas_call(
        first_sum_kernel, out_shape=[one] * 4,
        in_specs=[SM] + [VM] * 5, out_specs=[VM] * 4,
        scratch_shapes=[pltpu.VMEM((4, tiles, 8, B), f32)],
        compiler_params=PARAMS, name="first_sum")(z_now, own, up, down, up2, down2)
    plus, minus = shifted(plus, 4), shifted(minus, -4)
    far = lax.all_gather(far, "half")
    chunks = pl.pallas_call(
        second_sum_kernel, out_shape=tile_array(tms),
        in_specs=[SM, SM] + [VM] * 4, out_specs=VM,
        scratch_shapes=[pltpu.VMEM((2, 3 * tms, B), f32)],
        compiler_params=PARAMS, name="second_sum")(z_now, decays, mine, plus, minus, far)
    chunks = lax.all_to_all(chunks, "tm", 0, 0)
    chunks = pl.pallas_call(
        scan_kernel, out_shape=jax.ShapeDtypeStruct((2, tms, 4, B), f32), in_specs=[VM], out_specs=VM,
        compiler_params=PARAMS, name="scan")(chunks)
    chunks = lax.all_to_all(chunks.reshape(2 * tms, 4, B), ("side", "tm"), 0, 0)
    mine = pl.pallas_call(
        unpack_kernel, out_shape=one, in_specs=[VM], out_specs=VM,
        scratch_shapes=[pltpu.VMEM((2, 3 * tms, B), f32)],
        compiler_params=PARAMS, name="unpack")(chunks.reshape(2, tms, 4, B))
    pieces = lax.all_gather(mine, ("half", "quarter", "near"))
    keep, send = pl.pallas_call(
        solve_kernel,
        out_shape=[jax.ShapeDtypeStruct((share + 8, width), f32)] * 2,
        in_specs=[SM, VM], out_specs=[VM] * 2,
        scratch_shapes=[
            pltpu.VMEM((width, width), f32), pltpu.VMEM((width, width), f32),
            pltpu.VMEM((nb, B, B), f32), pltpu.VMEM((8, width), f32), pltpu.VMEM((8, width), f32)],
        compiler_params=PARAMS, name="solve")(z_now, pieces)
    got = lax.ppermute(send, "side", [(0, 1), (1, 0)])
    factor, state = pl.pallas_call(
        join_kernel,
        out_shape=[jax.ShapeDtypeStruct((segs, share, width), f32), jax.ShapeDtypeStruct((segs, share), f32)],
        in_specs=[SM, VM, VM], out_specs=[VM] * 2,
        compiler_params=PARAMS, name="join")(z_now, keep, got)
    return (factor, state)


def solution(mesh):
    count, tms = mesh.devices.shape
    paired = Mesh(mesh.devices.reshape(2, count // 8, 2, 2, tms), ROWS + ("tm",))
    in_specs = (P("tm", ROWS, None), P("tm", ROWS), P("tm"), P("tm"))
    out_specs = (P("tm", ROWS, None), P("tm", ROWS))
    return jax.shard_map(
        on_device, mesh=paired, in_specs=in_specs, out_specs=out_specs, check_vma=False
    )
```

```python
import functools
import jax
import jax.numpy as jnp
from jax import lax
from jax.experimental import pallas as pl
from jax.experimental.pallas import tpu as pltpu
from jax.sharding import Mesh, PartitionSpec as P

f32 = jnp.float32
B = 128
ROWS = ("half", "quarter", "near", "side")
HIGH = lax.Precision.HIGHEST
VM = pl.BlockSpec(memory_space=pltpu.VMEM)
SM = pl.BlockSpec(memory_space=pltpu.SMEM)
PARAMS = pltpu.CompilerParams(vmem_limit_bytes=48 << 20)


def block_list(nb):
    return [(b, c) for b in range(nb) for c in range(b, nb) if b < nb - 1]


def tile_array(*lead):
    return jax.ShapeDtypeStruct(tuple(lead) + (8, B), f32)


def spare_quarter():
    row = lax.broadcasted_iota(jnp.int32, (B, B), 0)
    col = lax.broadcasted_iota(jnp.int32, (B, B), 1)
    return (row >= B // 2) & (col < B // 2)


def swap_halves(block):
    return jnp.concatenate([block[B // 2:], block[:B // 2]], axis=0)


def pack_kernel(z_ref, jac_ref, rhs_ref, own, up, down, up2, down2, parts):
    z = z_ref[0]
    segs, rows, width = jac_ref.shape
    nb = width // B
    blocks = block_list(nb)
    last = segs * len(blocks)
    for p in range(4):
        for a in range(4):
            parts[p, a, last] = jnp.zeros((8, B), f32)
    grads = []
    spare = spare_quarter()
    for s in range(segs):
        jac = jac_ref[s]
        quarters = None
        for b in range(nb - 1, -1, -1):
            info = lax.dot_general(
                jac[:, b * B:(b + 1) * B], jac[:, b * B:],
                (((0,), (0,)), ((), ())), preferred_element_type=f32)
            if b == nb - 1:
                turned = pltpu.roll(info, B // 2, 1)
                quarters = [swap_halves(info), swap_halves(turned), turned]
                continue
            for c in range(b, nb):
                tile = s * len(blocks) + blocks.index((b, c))
                block = info[:, (c - b) * B:(c - b + 1) * B]
                if c == b:
                    block = jnp.where(spare, quarters[b], block)
                piece = block.reshape(4, 4, 8, B)
                for q in range(4):
                    p = lax.rem(q + 16 - z, 4)
                    for a in range(4):
                        parts[p, a, tile] = piece[a, q]
        grads.append(jnp.dot(rhs_ref[...], jac, preferred_element_type=f32)[s:s + 1])
    p = lax.rem(16 - z, 4)
    for s in range(segs):
        for b in range(nb):
            parts[p, 0, last, pl.ds(s * nb + b, 1), :] = grads[s][:, b * B:(b + 1) * B]
    own[...] = parts[0]
    up[...] = parts[1]
    up2[...] = parts[2, 0:2]
    down2[...] = parts[2, 2:4]
    down[...] = parts[3]


def first_sum_kernel(z_ref, own, up, down, up2, down2, mine, plus, minus, far, total):
    h = lax.div(z_ref[0], 4)
    near = own[...] + up[...] + down[...]
    total[0:2] = near[0:2] + up2[...]
    total[2:4] = near[2:4] + down2[...]
    mine[...] = total[h]
    plus[...] = total[lax.rem(h + 1, 4)]
    minus[...] = total[lax.rem(h + 3, 4)]
    far[...] = total[lax.rem(h + 2, 4)]


def second_sum_kernel(z_ref, decay_ref, mine, plus, minus, far, out, flat):
    total = (mine[...] + plus[...]) + (minus[...] + far[1 - lax.div(z_ref[0], 8)])
    half = (total.shape[0] - 1) // 2
    for s in range(2):
        flat[s, 0:8 * half] = total[s * half:(s + 1) * half].reshape(8 * half, B)
        flat[s, 8 * half:8 * half + 4] = total[2 * half, 4 * s:4 * s + 4]
        flat[s, 8 * half + 4:] = jnp.zeros((flat.shape[1] - 8 * half - 4, B), f32)
    for t in range(out.shape[0]):
        for s in range(2):
            out[t, 3 * s:3 * s + 3] = flat[s, 3 * t:3 * t + 3]
            out[t, 6 + s:7 + s] = jnp.full((1, B), decay_ref[s], f32)


def scan_kernel(chunks, out):
    now = jnp.zeros((3, B), f32)
    for t in range(chunks.shape[0]):
        for s in range(2):
            now = chunks[t, 6 + s:7 + s] * now + chunks[t, 3 * s:3 * s + 3]
            out[s, t, 0:3] = now
            out[s, t, 3:4] = jnp.zeros((1, B), f32)


def unpack_kernel(chunks, out, flat):
    half = (out.shape[0] - 1) // 2
    for g in range(2):
        for t in range(chunks.shape[1]):
            flat[g, 3 * t:3 * t + 3] = chunks[g, t, 0:3]
        out[g * half:(g + 1) * half] = flat[g, 0:8 * half].reshape(half, 8, B)
        out[2 * half, 4 * g:4 * g + 4] = flat[g, 8 * half:8 * half + 4]


def spread(row):
    return jnp.broadcast_to(row, (8, B))


def across(value, lane):
    return jnp.broadcast_to(value[:, lane:lane + 1], (8, B))


def invert_factor(rows, lane, sub, jobs):
    groups = len(rows)
    jobs = list(jobs)
    cols = [across(rows[0], m) for m in range(8)]
    for j in range(groups):
        o = 8 * j
        top = rows[j]
        more = j + 1 < groups
        inside = (lane >= o) & (lane < o + 8)
        a = {(r, m): spread(cols[m][r:r + 1]) for m in range(8) for r in range(m, 8)}
        if more:
            left = [across(rows[j + 1], o + m) for m in range(8)]
            cols = [across(rows[j + 1], o + 8 + m) for m in range(8)]
            after = jnp.where(inside, 0.0, rows[j + 1])
        d = []
        for m in range(8):
            unit = jnp.where(lane == o + m, 1.0, 0.0)
            d.append(jnp.where(inside, unit, spread(top[m:m + 1])))
        low, rs, u = {}, [], []
        for k in range(8):
            r = lax.rsqrt(a[k, k])
            rs.append(r)
            for m in range(k + 1, 8):
                low[m, k] = a[m, k] * r
            for m in range(k + 1, 8):
                for n in range(m, 8):
                    a[n, m] = a[n, m] - low[n, k] * low[m, k]
            u.append(d[k] * r)
            for m in range(k + 1, 8):
                d[m] = d[m] - low[m, k] * u[k]
            if more:
                col = left[k] * r
                for m in range(k + 1, 8):
                    left[m] = left[m] - col * low[m, k]
                for m in range(8):
                    cols[m] = cols[m] - col * spread(col[m:m + 1])
                after = after - col * u[k]
        if more:
            rows[j + 1] = after
        w = [None] * 8
        for m in range(7, -1, -1):
            acc = u[m]
            for k in range(7, m, -1):
                acc = acc - low[k, m] * w[k]
            w[m] = acc * rs[m]
        for i in range(j + 2, groups):
            old = rows[i]
            new = jnp.where(inside, 0.0, old)
            for m in range(7, -1, -1):
                new = new - across(old, o + m) * w[m]
            rows[i] = new
        merged = u[0]
        for m in range(1, 8):
            merged = jnp.where(sub == m, u[m], merged)
        rows[j] = merged
        if jobs:
            jobs.pop(0)()
    for job in jobs:
        job()
    return rows


def times(x, y):
    return jnp.dot(x, y, precision=HIGH, preferred_element_type=f32)


def left_transposed(x, y):
    return lax.dot_general(x, y, (((0,), (0,)), ((), ())), precision=HIGH, preferred_element_type=f32)


def right_transposed(x, y):
    return lax.dot_general(x, y, (((1,), (1,)), ((), ())), precision=HIGH, preferred_element_type=f32)


def solve_kernel(z_ref, pieces, keep, send, mat, upper, inv, vec, sol):
    z = z_ref[0]
    width = mat.shape[0]
    nb = width // B
    blocks = block_list(nb)
    nblk = len(blocks)
    lane = lax.broadcasted_iota(jnp.int32, (8, B), 1)
    sub = lax.broadcasted_iota(jnp.int32, (8, B), 0)
    row_i = lax.broadcasted_iota(jnp.int32, (B, B), 0)
    col_i = lax.broadcasted_iota(jnp.int32, (B, B), 1)
    vec[...] = jnp.zeros(vec.shape, f32)
    for i, (b, c) in enumerate(blocks):
        for h in range(pieces.shape[0]):
            for g in range(2):
                at = b * B + (2 * h + g) * 8
                mat[at:at + 8, c * B:(c + 1) * B] = pieces[h, g * nblk + i]
    for b in range(nb):
        vec[0:1, b * B:(b + 1) * B] = pieces[0, 2 * nblk, b:b + 1]

    def span(b):
        return slice(b * B, (b + 1) * B)

    def panel(b, c):
        upper[span(b), span(c)] = times(inv[b], mat[span(b), span(c)])

    def diagonal(b):
        block = times(inv[b], mat[span(b), span(b)])
        upper[span(b), span(b)] = jnp.where(col_i >= row_i, block, 0.0)
        if b:
            upper[span(b), 0:b * B] = jnp.zeros((B, b * B), f32)

    def trail(b, c, d):
        mat[span(c), span(d)] = mat[span(c), span(d)] - left_transposed(upper[span(b), span(c)], upper[span(b), span(d)])

    def forward(b):
        sol[:, span(b)] = right_transposed(vec[:, span(b)], inv[b])

    def advance(b, c):
        vec[:, span(c)] = vec[:, span(c)] - times(sol[:, span(b)], upper[span(b), span(c)])

    spare = spare_quarter()
    first, second, third = [mat[span(b), span(b)] for b in range(3)]
    right = col_i >= B // 2
    mat[span(3), span(3)] = jnp.where(
        row_i < B // 2,
        jnp.where(right, pltpu.roll(swap_halves(second), B // 2, 1), swap_halves(first)),
        pltpu.roll(third, B // 2, 1))

    def mirror(b):
        block = mat[span(b), span(b)]
        mat[span(b), span(b)] = jnp.where(spare, block.T, block)

    mirror(0)
    jobs = [functools.partial(mirror, b) for b in range(1, nb)]
    for b in range(nb):
        rows = [mat[b * B + 8 * i:b * B + 8 * i + 8, span(b)] for i in range(B // 8)]
        rows = invert_factor(rows, lane, sub, jobs)
        inv[b] = jnp.where(col_i <= row_i, jnp.concatenate(rows, axis=0), 0.0)
        jobs = []
        if b + 1 < nb:
            panel(b, b + 1)
            trail(b, b + 1, b + 1)
        for c in range(b + 2, nb):
            jobs.append(functools.partial(panel, b, c))
        for c in range(b + 1, nb):
            for d in range(c, nb):
                if d > b + 1:
                    jobs.append(functools.partial(trail, b, c, d))
        jobs.append(functools.partial(diagonal, b))
        jobs.append(functools.partial(forward, b))
        for c in range(b + 1, nb):
            jobs.append(functools.partial(advance, b, c))
    for job in jobs:
        job()

    for b in range(nb - 1, -1, -1):
        y = sol[:, span(b)]
        if b + 1 < nb:
            y = y - right_transposed(vec[:, (b + 1) * B:], upper[span(b), (b + 1) * B:])
        vec[:, span(b)] = times(y, inv[b])
    share = keep.shape[0] - 8
    other = z + 1 - 2 * lax.rem(z, 2)
    keep[0:share] = upper[pl.ds(pl.multiple_of(z * share, share), share), :]
    send[0:share] = upper[pl.ds(pl.multiple_of(other * share, share), share), :]
    keep[share:] = vec[...]
    send[share:] = vec[...]


def join_kernel(z_ref, keep, got, factor, state):
    share = factor.shape[1]
    s = lax.rem(z_ref[0], 2)
    factor[s] = keep[0:share]
    factor[1 - s] = got[0:share]
    first = jnp.where(s == 0, keep[share:], got[share:])
    second = jnp.where(s == 0, got[share:], keep[share:])
    left = lax.rem(first.shape[1] - z_ref[0] * share, first.shape[1])
    state[0:1] = pltpu.roll(first, left, 1)[0:1, 0:share]
    state[1:2] = pltpu.roll(second, left, 1)[0:1, 0:share]


def shifted(value, by):
    count = lax.axis_size(ROWS)
    return lax.ppermute(value, ROWS, [(i, (i + by) % count) for i in range(count)])


def on_device(jacobian, rhs, forget, restart):
    segs, rows, width = jacobian.shape
    nb = width // B
    tiles = segs * len(block_list(nb)) + 1
    tms = lax.axis_size("tm")
    z = lax.axis_index(ROWS)
    z_now = z.astype(jnp.int32).reshape(1)
    share = width // lax.axis_size(ROWS)
    decays = forget * (1.0 - 0.2 * restart.astype(f32))

    four, two, one = tile_array(4, tiles), tile_array(2, tiles), tile_array(tiles)
    own, up, down, up2, down2 = pl.pallas_call(
        pack_kernel, out_shape=[four, four, four, two, two],
        in_specs=[SM, VM, VM], out_specs=[VM] * 5,
        scratch_shapes=[pltpu.VMEM((4, 4, tiles, 8, B), f32)],
        compiler_params=PARAMS, name="pack")(z_now, jacobian, rhs)
    up, down, up2, down2 = shifted(up, 1), shifted(down, -1), shifted(up2, 2), shifted(down2, -2)
    mine, plus, minus, far = pl.pallas_call(
        first_sum_kernel, out_shape=[one] * 4,
        in_specs=[SM] + [VM] * 5, out_specs=[VM] * 4,
        scratch_shapes=[pltpu.VMEM((4, tiles, 8, B), f32)],
        compiler_params=PARAMS, name="first_sum")(z_now, own, up, down, up2, down2)
    plus, minus = shifted(plus, 4), shifted(minus, -4)
    far = lax.all_gather(far, "half")
    chunks = pl.pallas_call(
        second_sum_kernel, out_shape=tile_array(tms),
        in_specs=[SM, SM] + [VM] * 4, out_specs=VM,
        scratch_shapes=[pltpu.VMEM((2, 3 * tms, B), f32)],
        compiler_params=PARAMS, name="second_sum")(z_now, decays, mine, plus, minus, far)
    chunks = lax.all_to_all(chunks, "tm", 0, 0)
    chunks = pl.pallas_call(
        scan_kernel, out_shape=jax.ShapeDtypeStruct((2, tms, 4, B), f32), in_specs=[VM], out_specs=VM,
        compiler_params=PARAMS, name="scan")(chunks)
    chunks = lax.all_to_all(chunks.reshape(2 * tms, 4, B), ("side", "tm"), 0, 0)
    mine = pl.pallas_call(
        unpack_kernel, out_shape=one, in_specs=[VM], out_specs=VM,
        scratch_shapes=[pltpu.VMEM((2, 3 * tms, B), f32)],
        compiler_params=PARAMS, name="unpack")(chunks.reshape(2, tms, 4, B))
    pieces = lax.all_gather(mine, ("half", "quarter", "near"))
    keep, send = pl.pallas_call(
        solve_kernel,
        out_shape=[jax.ShapeDtypeStruct((share + 8, width), f32)] * 2,
        in_specs=[SM, VM], out_specs=[VM] * 2,
        scratch_shapes=[
            pltpu.VMEM((width, width), f32), pltpu.VMEM((width, width), f32),
            pltpu.VMEM((nb, B, B), f32), pltpu.VMEM((8, width), f32), pltpu.VMEM((8, width), f32)],
        compiler_params=PARAMS, name="solve")(z_now, pieces)
    got = lax.ppermute(send, "side", [(0, 1), (1, 0)])
    factor, state = pl.pallas_call(
        join_kernel,
        out_shape=[jax.ShapeDtypeStruct((segs, share, width), f32), jax.ShapeDtypeStruct((segs, share), f32)],
        in_specs=[SM, VM, VM], out_specs=[VM] * 2,
        compiler_params=PARAMS, name="join")(z_now, keep, got)
    return (factor, state)


def solution(mesh):
    count, tms = mesh.devices.shape
    paired = Mesh(mesh.devices.reshape(2, count // 8, 2, 2, tms), ROWS + ("tm",))
    in_specs = (P("tm", ROWS, None), P("tm", ROWS), P("tm"), P("tm"))
    out_specs = (P("tm", ROWS, None), P("tm", ROWS))
    return jax.shard_map(
        on_device, mesh=paired, in_specs=in_specs, out_specs=out_specs, check_vma=False
    )
```

```python
import functools
import jax
import jax.numpy as jnp
from jax import lax
from jax.experimental import pallas as pl
from jax.experimental.pallas import tpu as pltpu
from jax.sharding import Mesh, PartitionSpec as P

f32 = jnp.float32
B = 128
ROWS = ("half", "quarter", "near", "side")
HIGH = lax.Precision.HIGHEST
VM = pl.BlockSpec(memory_space=pltpu.VMEM)
SM = pl.BlockSpec(memory_space=pltpu.SMEM)
PARAMS = pltpu.CompilerParams(vmem_limit_bytes=48 << 20)


def block_list(nb):
    return [(b, c) for b in range(nb) for c in range(b, nb) if b < nb - 1]


def tile_array(*lead):
    return jax.ShapeDtypeStruct(tuple(lead) + (8, B), f32)


def spare_quarter():
    row = lax.broadcasted_iota(jnp.int32, (B, B), 0)
    col = lax.broadcasted_iota(jnp.int32, (B, B), 1)
    return (row >= B // 2) & (col < B // 2)


def swap_halves(block):
    return jnp.concatenate([block[B // 2:], block[:B // 2]], axis=0)


def pack_kernel(z_ref, jac_ref, rhs_ref, own, up, down, up2, down2, parts):
    z = z_ref[0]
    segs, rows, width = jac_ref.shape
    nb = width // B
    blocks = block_list(nb)
    last = segs * len(blocks)
    for p in range(4):
        for a in range(4):
            parts[p, a, last] = jnp.zeros((8, B), f32)
    grads = []
    spare = spare_quarter()
    for s in range(segs):
        jac = jac_ref[s]
        quarters = None
        for b in range(nb - 1, -1, -1):
            info = lax.dot_general(
                jac[:, b * B:(b + 1) * B], jac[:, b * B:],
                (((0,), (0,)), ((), ())), preferred_element_type=f32)
            if b == nb - 1:
                turned = pltpu.roll(info, B // 2, 1)
                quarters = [swap_halves(info), swap_halves(turned), turned]
                continue
            for c in range(b, nb):
                tile = s * len(blocks) + blocks.index((b, c))
                block = info[:, (c - b) * B:(c - b + 1) * B]
                if c == b:
                    block = jnp.where(spare, quarters[b], block)
                piece = block.reshape(4, 4, 8, B)
                for q in range(4):
                    p = lax.rem(q + 16 - z, 4)
                    for a in range(4):
                        parts[p, a, tile] = piece[a, q]
        grads.append(jnp.dot(rhs_ref[...], jac, preferred_element_type=f32)[s:s + 1])
    p = lax.rem(16 - z, 4)
    for s in range(segs):
        for b in range(nb):
            parts[p, 0, last, pl.ds(s * nb + b, 1), :] = grads[s][:, b * B:(b + 1) * B]
    own[...] = parts[0]
    up[...] = parts[1]
    up2[...] = parts[2, 0:2]
    down2[...] = parts[2, 2:4]
    down[...] = parts[3]


def first_sum_kernel(z_ref, own, up, down, up2, down2, mine, plus, minus, far, total):
    h = lax.div(z_ref[0], 4)
    near = own[...] + up[...] + down[...]
    total[0:2] = near[0:2] + up2[...]
    total[2:4] = near[2:4] + down2[...]
    mine[...] = total[h]
    plus[...] = total[lax.rem(h + 1, 4)]
    minus[...] = total[lax.rem(h + 3, 4)]
    far[...] = total[lax.rem(h + 2, 4)]


def second_sum_kernel(z_ref, decay_ref, mine, plus, minus, far, out, flat):
    total = (mine[...] + plus[...]) + (minus[...] + far[1 - lax.div(z_ref[0], 8)])
    half = (total.shape[0] - 1) // 2
    for s in range(2):
        flat[s, 0:8 * half] = total[s * half:(s + 1) * half].reshape(8 * half, B)
        flat[s, 8 * half:8 * half + 4] = total[2 * half, 4 * s:4 * s + 4]
        flat[s, 8 * half + 4:] = jnp.zeros((flat.shape[1] - 8 * half - 4, B), f32)
    for t in range(out.shape[0]):
        for s in range(2):
            out[t, 3 * s:3 * s + 3] = flat[s, 3 * t:3 * t + 3]
            out[t, 6 + s:7 + s] = jnp.full((1, B), decay_ref[s], f32)


def scan_kernel(chunks, out):
    now = jnp.zeros((3, B), f32)
    for t in range(chunks.shape[0]):
        for s in range(2):
            now = chunks[t, 6 + s:7 + s] * now + chunks[t, 3 * s:3 * s + 3]
            out[s, t, 0:3] = now
            out[s, t, 3:4] = jnp.zeros((1, B), f32)


def unpack_kernel(chunks, out, flat):
    half = (out.shape[0] - 1) // 2
    for g in range(2):
        for t in range(chunks.shape[1]):
            flat[g, 3 * t:3 * t + 3] = chunks[g, t, 0:3]
        out[g * half:(g + 1) * half] = flat[g, 0:8 * half].reshape(half, 8, B)
        out[2 * half, 4 * g:4 * g + 4] = flat[g, 8 * half:8 * half + 4]


def spread(row):
    return jnp.broadcast_to(row, (8, B))


def across(value, lane):
    return jnp.broadcast_to(value[:, lane:lane + 1], (8, B))


def invert_factor(rows, lane, sub, jobs):
    groups = len(rows)
    jobs = list(jobs)
    cols = [across(rows[0], m) for m in range(8)]
    for j in range(groups):
        o = 8 * j
        top = rows[j]
        more = j + 1 < groups
        inside = (lane >= o) & (lane < o + 8)
        a = {(r, m): spread(cols[m][r:r + 1]) for m in range(8) for r in range(m, 8)}
        if more:
            left = [across(rows[j + 1], o + m) for m in range(8)]
            cols = [across(rows[j + 1], o + 8 + m) for m in range(8)]
            after = jnp.where(inside, 0.0, rows[j + 1])
        d = []
        for m in range(8):
            unit = jnp.where(lane == o + m, 1.0, 0.0)
            d.append(jnp.where(inside, unit, spread(top[m:m + 1])))
        low, rs, u = {}, [], []
        for k in range(8):
            r = lax.rsqrt(a[k, k])
            rs.append(r)
            for m in range(k + 1, 8):
                low[m, k] = a[m, k] * r
            for m in range(k + 1, 8):
                for n in range(m, 8):
                    a[n, m] = a[n, m] - low[n, k] * low[m, k]
            u.append(d[k] * r)
            for m in range(k + 1, 8):
                d[m] = d[m] - low[m, k] * u[k]
            if more:
                col = left[k] * r
                for m in range(k + 1, 8):
                    left[m] = left[m] - col * low[m, k]
                for m in range(8):
                    cols[m] = cols[m] - col * spread(col[m:m + 1])
                after = after - col * u[k]
        if more:
            rows[j + 1] = after
        w = [None] * 8
        for m in range(7, -1, -1):
            acc = u[m]
            for k in range(7, m, -1):
                acc = acc - low[k, m] * w[k]
            w[m] = acc * rs[m]
        for i in range(j + 2, groups):
            old = rows[i]
            new = jnp.where(inside, 0.0, old)
            for m in range(7, -1, -1):
                new = new - across(old, o + m) * w[m]
            rows[i] = new
        merged = u[0]
        for m in range(1, 8):
            merged = jnp.where(sub == m, u[m], merged)
        rows[j] = merged
        if jobs:
            jobs.pop(0)()
    for job in jobs:
        job()
    return rows


def times(x, y):
    return jnp.dot(x, y, precision=HIGH, preferred_element_type=f32)


def left_transposed(x, y):
    return lax.dot_general(x, y, (((0,), (0,)), ((), ())), precision=HIGH, preferred_element_type=f32)


def right_transposed(x, y):
    return lax.dot_general(x, y, (((1,), (1,)), ((), ())), precision=HIGH, preferred_element_type=f32)


def solve_kernel(z_ref, pieces, keep, send, mat, upper, inv, vec, sol):
    z = z_ref[0]
    width = mat.shape[0]
    nb = width // B
    blocks = block_list(nb)
    nblk = len(blocks)
    lane = lax.broadcasted_iota(jnp.int32, (8, B), 1)
    sub = lax.broadcasted_iota(jnp.int32, (8, B), 0)
    row_i = lax.broadcasted_iota(jnp.int32, (B, B), 0)
    col_i = lax.broadcasted_iota(jnp.int32, (B, B), 1)
    vec[...] = jnp.zeros(vec.shape, f32)
    for i, (b, c) in enumerate(blocks):
        for h in range(pieces.shape[0]):
            for g in range(2):
                at = b * B + (2 * h + g) * 8
                mat[at:at + 8, c * B:(c + 1) * B] = pieces[h, g * nblk + i]
    for b in range(nb):
        vec[0:1, b * B:(b + 1) * B] = pieces[0, 2 * nblk, b:b + 1]

    def span(b, end=None):
        return slice(b * B, (b + 1 if end is None else end) * B)

    def panel(b, c, end):
        upper[span(b), span(c, end)] = times(inv[b], mat[span(b), span(c, end)])

    def diagonal(b):
        block = times(inv[b], mat[span(b), span(b)])
        upper[span(b), span(b)] = jnp.where(col_i >= row_i, block, 0.0)
        if b:
            upper[span(b), 0:b * B] = jnp.zeros((B, b * B), f32)

    def trail(b, c, d, end):
        mat[span(c), span(d, end)] = mat[span(c), span(d, end)] - left_transposed(
            upper[span(b), span(c)], upper[span(b), span(d, end)])

    def forward(b):
        sol[:, span(b)] = right_transposed(vec[:, span(b)], inv[b])

    def advance(b):
        rest = span(b + 1, nb)
        vec[:, rest] = vec[:, rest] - times(sol[:, span(b)], upper[span(b), rest])

    spare = spare_quarter()
    first, second, third = [mat[span(b), span(b)] for b in range(3)]
    right = col_i >= B // 2
    mat[span(3), span(3)] = jnp.where(
        row_i < B // 2,
        jnp.where(right, pltpu.roll(swap_halves(second), B // 2, 1), swap_halves(first)),
        pltpu.roll(third, B // 2, 1))

    def mirror(b):
        block = mat[span(b), span(b)]
        mat[span(b), span(b)] = jnp.where(spare, block.T, block)

    mirror(0)
    jobs = [functools.partial(mirror, b) for b in range(1, nb)]
    for b in range(nb):
        rows = [mat[b * B + 8 * i:b * B + 8 * i + 8, span(b)] for i in range(B // 8)]
        rows = invert_factor(rows, lane, sub, jobs)
        inv[b] = jnp.where(col_i <= row_i, jnp.concatenate(rows, axis=0), 0.0)
        jobs = []
        if b + 1 < nb:
            panel(b, b + 1, b + 2)
            trail(b, b + 1, b + 1, b + 2)
        jobs.append(functools.partial(forward, b))
        if b + 2 < nb:
            jobs.append(functools.partial(panel, b, b + 2, nb))
            jobs.append(functools.partial(trail, b, b + 1, b + 2, nb))
        for c in range(b + 2, nb):
            jobs.append(functools.partial(trail, b, c, c, nb))
        if b + 1 < nb:
            jobs.append(functools.partial(advance, b))
        jobs.append(functools.partial(diagonal, b))
    for job in jobs:
        job()

    for b in range(nb - 1, -1, -1):
        y = sol[:, span(b)]
        if b + 1 < nb:
            y = y - right_transposed(vec[:, (b + 1) * B:], upper[span(b), (b + 1) * B:])
        vec[:, span(b)] = times(y, inv[b])
    share = keep.shape[0] - 8
    other = z + 1 - 2 * lax.rem(z, 2)
    keep[0:share] = upper[pl.ds(pl.multiple_of(z * share, share), share), :]
    send[0:share] = upper[pl.ds(pl.multiple_of(other * share, share), share), :]
    keep[share:] = vec[...]
    send[share:] = vec[...]


def join_kernel(z_ref, keep, got, factor, state):
    share = factor.shape[1]
    s = lax.rem(z_ref[0], 2)
    factor[s] = keep[0:share]
    factor[1 - s] = got[0:share]
    first = jnp.where(s == 0, keep[share:], got[share:])
    second = jnp.where(s == 0, got[share:], keep[share:])
    left = lax.rem(first.shape[1] - z_ref[0] * share, first.shape[1])
    state[0:1] = pltpu.roll(first, left, 1)[0:1, 0:share]
    state[1:2] = pltpu.roll(second, left, 1)[0:1, 0:share]


def shifted(value, by):
    count = lax.axis_size(ROWS)
    return lax.ppermute(value, ROWS, [(i, (i + by) % count) for i in range(count)])


def on_device(jacobian, rhs, forget, restart):
    segs, rows, width = jacobian.shape
    nb = width // B
    tiles = segs * len(block_list(nb)) + 1
    tms = lax.axis_size("tm")
    z = lax.axis_index(ROWS)
    z_now = z.astype(jnp.int32).reshape(1)
    share = width // lax.axis_size(ROWS)
    decays = forget * (1.0 - 0.2 * restart.astype(f32))

    four, two, one = tile_array(4, tiles), tile_array(2, tiles), tile_array(tiles)
    own, up, down, up2, down2 = pl.pallas_call(
        pack_kernel, out_shape=[four, four, four, two, two],
        in_specs=[SM, VM, VM], out_specs=[VM] * 5,
        scratch_shapes=[pltpu.VMEM((4, 4, tiles, 8, B), f32)],
        compiler_params=PARAMS, name="pack")(z_now, jacobian, rhs)
    up, down, up2, down2 = shifted(up, 1), shifted(down, -1), shifted(up2, 2), shifted(down2, -2)
    mine, plus, minus, far = pl.pallas_call(
        first_sum_kernel, out_shape=[one] * 4,
        in_specs=[SM] + [VM] * 5, out_specs=[VM] * 4,
        scratch_shapes=[pltpu.VMEM((4, tiles, 8, B), f32)],
        compiler_params=PARAMS, name="first_sum")(z_now, own, up, down, up2, down2)
    plus, minus = shifted(plus, 4), shifted(minus, -4)
    far = lax.all_gather(far, "half")
    chunks = pl.pallas_call(
        second_sum_kernel, out_shape=tile_array(tms),
        in_specs=[SM, SM] + [VM] * 4, out_specs=VM,
        scratch_shapes=[pltpu.VMEM((2, 3 * tms, B), f32)],
        compiler_params=PARAMS, name="second_sum")(z_now, decays, mine, plus, minus, far)
    chunks = lax.all_to_all(chunks, "tm", 0, 0)
    chunks = pl.pallas_call(
        scan_kernel, out_shape=jax.ShapeDtypeStruct((2, tms, 4, B), f32), in_specs=[VM], out_specs=VM,
        compiler_params=PARAMS, name="scan")(chunks)
    chunks = lax.all_to_all(chunks.reshape(2 * tms, 4, B), ("side", "tm"), 0, 0)
    mine = pl.pallas_call(
        unpack_kernel, out_shape=one, in_specs=[VM], out_specs=VM,
        scratch_shapes=[pltpu.VMEM((2, 3 * tms, B), f32)],
        compiler_params=PARAMS, name="unpack")(chunks.reshape(2, tms, 4, B))
    pieces = lax.all_gather(mine, ("half", "quarter", "near"))
    keep, send = pl.pallas_call(
        solve_kernel,
        out_shape=[jax.ShapeDtypeStruct((share + 8, width), f32)] * 2,
        in_specs=[SM, VM], out_specs=[VM] * 2,
        scratch_shapes=[
            pltpu.VMEM((width, width), f32), pltpu.VMEM((width, width), f32),
            pltpu.VMEM((nb, B, B), f32), pltpu.VMEM((8, width), f32), pltpu.VMEM((8, width), f32)],
        compiler_params=PARAMS, name="solve")(z_now, pieces)
    got = lax.ppermute(send, "side", [(0, 1), (1, 0)])
    factor, state = pl.pallas_call(
        join_kernel,
        out_shape=[jax.ShapeDtypeStruct((segs, share, width), f32), jax.ShapeDtypeStruct((segs, share), f32)],
        in_specs=[SM, VM, VM], out_specs=[VM] * 2,
        compiler_params=PARAMS, name="join")(z_now, keep, got)
    return (factor, state)


def solution(mesh):
    count, tms = mesh.devices.shape
    paired = Mesh(mesh.devices.reshape(2, count // 8, 2, 2, tms), ROWS + ("tm",))
    in_specs = (P("tm", ROWS, None), P("tm", ROWS), P("tm"), P("tm"))
    out_specs = (P("tm", ROWS, None), P("tm", ROWS))
    return jax.shard_map(
        on_device, mesh=paired, in_specs=in_specs, out_specs=out_specs, check_vma=False
    )
```
